32 devices in a mesh: wide: 4 (over z), blk: 8 (over y, x, core).
Axes of the slice: x: 2, y: 2, z: 4, core: 2. Of those that a mesh axis runs over, the one named last changes fastest.
Arguments:
- rhs: float32 [131072, 256], P(('wide', 'blk'))
- near_blocks: bfloat16 [131072, 1536], P(('wide', 'blk')), may hold values from -0.078125 to 0.078125
- source_basis: bfloat16 [131072, 64], P(('wide', 'blk')), may hold values from -0.5 to 0.5
- target_basis: bfloat16 [131072, 64], P(('wide', 'blk')), may hold values from -0.375 to 0.375
- far_coupling: bfloat16 [1024, 1, 64, 64], P(('wide', 'blk')), may hold values from -0.75 to 0.75
- send_ids: int32 [32, 32, 1], P(('wide', 'blk')), may hold values from 0 to 31
- far_list: int32 [32, 32], P(('wide', 'blk')), may hold values from 0 to 31, each once within a row
Outputs:
- solution: float32 [131072, 256], P(('wide', 'blk'))
- residual: float32 [131072, 256], P(('wide', 'blk'))
The draws below stay inside these ranges and needn't reach their ends.
Inputs may be any that keep to these rules, and one draw needn't show every extreme that they name: Each row of far_list names each received slot 0 to 31 exactly once.
All inputs are finite; a program needn't handle non-finite values.
Results may differ from the reference program's by a relative error of at most 0.0035.
The reference program's roundings to bfloat16 on the way (of `vb`, `coef` and `trans`) count: a program that leaves them out, or rounds other values in their place, can miss the bound.
Values may be sent and summed in bfloat16 or wider, within the bound.
A program may use at most 128 MiB of HBM per device.

```python
import jax
import jax.numpy as jnp
from jax import lax

ROWS = 4096
NRHS = 256
NEAR = 1024
HALO = 256
LEAF = 128
RANK = 64
SLOT = 1
ITERS = 2
LD = 32
FAN = 1
TOTAL = 131072
LEAVES = 1024
N_WIDE = 4
N_BLK = 8
DEVICES = 32


def draw_rhs(key, part):
    total = DEVICES * ROWS
    owner = (jnp.arange(total, dtype=jnp.int32) // ROWS).astype(jnp.float32)
    rising = jnp.exp(jnp.log(3.0) * owner / max(DEVICES - 1, 1))[:, None]
    values = jax.random.normal(jax.random.fold_in(key, 7), (total, NRHS), jnp.float32) * rising
    return jnp.clip(values, -12.0, 12.0)


def set_ends(result, rng, smallest, high):
    extent = result.shape
    place = [jax.random.randint(jax.random.fold_in(rng, axis), (), 0, extent[axis]) for axis in range(len(extent))]
    result = result.at[tuple(place)].set(smallest)
    longest = extent.index(max(extent))
    place[longest] = (place[longest] + 1) % extent[longest]
    return result.at[tuple(place)].set(high)


def level_of(stream_key, extent, shards, least, high):
    def one(dim, shards_of):
        heights = jax.random.uniform(jax.random.fold_in(jax.random.fold_in(stream_key, 6), dim), (shards_of,), jnp.float32, least / len(shards), high / len(shards))
        return jnp.repeat(jnp.exp(heights), extent[dim] // shards_of).reshape((-1,) + (1,) * (len(extent) - dim - 1))

    gain = one(*shards[0])
    for cut in shards[1:]:
        gain = gain * one(*cut)
    return gain


def noise(rng, dims, scale, reach, cuts=(), kind=jnp.bfloat16):
    factor_of = level_of(rng, dims, cuts, -0.22, 0.18) if cuts else 1.0
    array = jax.random.normal(rng, dims, jnp.float32) * scale * factor_of
    return jnp.minimum(jnp.maximum(array, -reach), reach).astype(kind)


def setup_inputs(seed: int = 0) -> dict:
    keys = jax.random.split(jax.random.key(seed), 8)
    return {
        "rhs": draw_rhs(jax.random.fold_in(keys[7], 71), 0),
        "near_blocks": noise(keys[1], (TOTAL, NEAR + 2 * HALO), (4 * (NEAR + 2 * HALO)) ** -0.5, 0.078125, ((0, 32),)),
        "source_basis": noise(keys[2], (TOTAL, RANK), LEAF ** -0.5, 0.5, ((0, 32),)),
        "target_basis": noise(keys[3], (TOTAL, RANK), (4 * RANK) ** -0.5, 0.375, ((0, 32),)),
        "far_coupling": noise(keys[4], (LEAVES, FAN, RANK, RANK), (FAN * RANK) ** -0.5, 0.75, ((0, 32),)),
        "send_ids": set_ends(jax.random.randint(keys[5], (DEVICES, DEVICES, SLOT), 0, LD), jax.random.fold_in(keys[5], 1), 0, LD - 1).astype(jnp.int32),
        "far_list": jax.vmap(lambda own: jax.random.permutation(own, DEVICES * SLOT))(jax.random.split(keys[6], DEVICES)).reshape((DEVICES, LD * FAN)).astype(jnp.int32),
    }


def near_apply(near_rows, ext):
    outs = []
    for j in range(ROWS // NEAR):
        outs.append(jnp.dot(near_rows[j * NEAR:(j + 1) * NEAR].astype(jnp.float32), ext[j * NEAR:j * NEAR + NEAR + 2 * HALO].astype(jnp.float32), preferred_element_type=jnp.float32))
    return jnp.concatenate(outs, axis=0)

def reference(rhs, near_blocks, source_basis, target_basis, far_coupling, send_ids, far_list):
    fanout = far_list.shape[1] // LD

    def apply(resid):
        vb = resid.astype(jnp.bfloat16)
        grid = vb.reshape(N_WIDE, N_BLK, ROWS, NRHS)
        ext_all = jnp.concatenate([jnp.roll(grid, 1, axis=1)[:, :, ROWS - HALO:], grid, jnp.roll(grid, -1, axis=1)[:, :, :HALO]], axis=2)
        ext_all = ext_all.reshape(DEVICES, ROWS + 2 * HALO, NRHS)
        basis = source_basis.astype(jnp.float32).reshape(DEVICES * LD, LEAF, RANK)
        coef = jnp.einsum('lia,lis->las', basis, vb.astype(jnp.float32).reshape(DEVICES * LD, LEAF, NRHS))
        coef = coef.astype(jnp.bfloat16).reshape(DEVICES, LD, RANK, NRHS)
        sources = jnp.arange(DEVICES, dtype=jnp.int32)[:, None]

        def one_device(device):
            received = coef[sources, send_ids[:, device, :]].reshape(DEVICES * SLOT, RANK, NRHS)
            picked = received[far_list[device]].reshape(LD, fanout, RANK, NRHS)
            coupling = lax.dynamic_slice_in_dim(far_coupling, device * LD, LD, 0)
            trans = jnp.einsum('lfab,lfbs->las', coupling.astype(jnp.float32), picked.astype(jnp.float32)).astype(jnp.bfloat16)
            target = lax.dynamic_slice_in_dim(target_basis, device * ROWS, ROWS, 0).reshape(LD, LEAF, RANK)
            far = jnp.einsum('lia,las->lis', target.astype(jnp.float32), trans.astype(jnp.float32)).reshape(ROWS, NRHS)
            near_rows = lax.dynamic_slice_in_dim(near_blocks, device * ROWS, ROWS, 0)
            return near_apply(near_rows, ext_all[device]) + far
        extra = lax.map(one_device, jnp.arange(DEVICES, dtype=jnp.int32))
        return resid + extra.reshape(DEVICES * ROWS, NRHS)
    solution = jnp.zeros_like(rhs)
    residual = rhs
    for step in range(ITERS):
        image = apply(residual)
        gram = jnp.einsum('rs,rt->st', image, image, precision=lax.Precision.HIGHEST)
        proj = jnp.einsum('rs,rt->st', image, residual, precision=lax.Precision.HIGHEST)
        factor = jnp.linalg.cholesky(gram)
        alpha = jax.scipy.linalg.cho_solve((factor, True), proj)
        solution = solution + jnp.dot(residual, alpha, precision=lax.Precision.HIGHEST)
        residual = residual - jnp.dot(image, alpha, precision=lax.Precision.HIGHEST)
    return (solution, residual)
```

```python
import functools

import jax
import jax.numpy as jnp
from jax import lax
from jax.experimental import pallas as pl
from jax.experimental.pallas import tpu as pltpu
from jax.sharding import PartitionSpec as P

NEAR = 1024
HALO = 256
LEAF = 128
ITERS = 2


def with_halo(value, sides, width):
    for axis, dim in sides:
        count, length = (lax.axis_size(axis), value.shape[dim])
        up = [(i, (i + 1) % count) for i in range(count)]
        down = [(j, i) for i, j in up]
        last = lax.slice_in_dim(value, length - width, length, axis=dim)
        first = lax.slice_in_dim(value, 0, width, axis=dim)
        before = lax.ppermute(last, axis, up)
        after = lax.ppermute(first, axis, down)
        value = jnp.concatenate([before, value, after], axis=dim)
    return value


def near_apply(near_rows, ext):
    outs = []
    for j in range(near_rows.shape[0] // NEAR):
        outs.append(
            jnp.dot(
                near_rows[j * NEAR : (j + 1) * NEAR],
                ext[j * NEAR : j * NEAR + NEAR + 2 * HALO],
                preferred_element_type=jnp.float32,
            )
        )
    return jnp.concatenate(outs, axis=0)


def dot32(a, b):
    return jnp.dot(a, b, precision=lax.Precision.HIGHEST, preferred_element_type=jnp.float32)


def sum_kernel(n, n_blk, part_ref, out_ref, landed, total, sent, got, sent2, got2):
    me = lax.axis_index("wide") * n_blk + lax.axis_index("blk")
    chunk = part_ref.shape[0] // n

    def peer_of(d):
        return lax.rem(me + d, n)

    def place(p):
        return {"wide": p // n_blk, "blk": lax.rem(p, n_blk)}

    def rows(p):
        return pl.ds(pl.multiple_of(p * chunk, chunk), chunk)

    barrier = pltpu.get_barrier_semaphore()

    def greet(d, c):
        pl.semaphore_signal(barrier, inc=1, device_id=place(peer_of(d)), device_id_type=pl.DeviceIdType.MESH)
        return c

    lax.fori_loop(1, n, greet, 0)
    pl.semaphore_wait(barrier, n - 1)

    def scatter(d):
        p = peer_of(d)
        return pltpu.make_async_remote_copy(
            src_ref=part_ref.at[rows(p)],
            dst_ref=landed.at[rows(me)],
            send_sem=sent.at[d],
            recv_sem=got.at[me],
            device_id=place(p),
            device_id_type=pl.DeviceIdType.MESH,
        )

    def gather(d):
        p = peer_of(d)
        return pltpu.make_async_remote_copy(
            src_ref=total.at[rows(me)],
            dst_ref=total.at[rows(me)],
            send_sem=sent2.at[d],
            recv_sem=got2.at[me],
            device_id=place(p),
            device_id_type=pl.DeviceIdType.MESH,
        )

    def arrived(ref, sems, d):
        p = peer_of(d)
        return pltpu.make_async_remote_copy(
            src_ref=ref.at[rows(p)],
            dst_ref=ref.at[rows(p)],
            send_sem=sent.at[d],
            recv_sem=sems.at[p],
            device_id=place(p),
            device_id_type=pl.DeviceIdType.MESH,
        )

    def start1(d, c):
        scatter(d).start()
        return c

    lax.fori_loop(1, n, start1, 0)

    def add(d, acc):
        arrived(landed, got, d).wait_recv()
        return acc + landed[rows(peer_of(d))]

    acc = lax.fori_loop(1, n, add, part_ref[rows(me)])
    total[rows(me)] = acc

    def start2(d, c):
        gather(d).start()
        return c

    lax.fori_loop(1, n, start2, 0)

    def drain(d, c):
        scatter(d).wait_send()
        gather(d).wait_send()
        arrived(total, got2, d).wait_recv()
        return c

    lax.fori_loop(1, n, drain, 0)
    out_ref[...] = total[...]


def sum_over_devices(part, n, n_blk):
    return pl.pallas_call(
        functools.partial(sum_kernel, n, n_blk),
        out_shape=jax.ShapeDtypeStruct(part.shape, part.dtype),
        in_specs=[pl.BlockSpec(memory_space=pltpu.VMEM)],
        out_specs=pl.BlockSpec(memory_space=pltpu.VMEM),
        scratch_shapes=[
            pltpu.VMEM(part.shape, part.dtype),
            pltpu.VMEM(part.shape, part.dtype),
            pltpu.SemaphoreType.DMA((n,)),
            pltpu.SemaphoreType.DMA((n,)),
            pltpu.SemaphoreType.DMA((n,)),
            pltpu.SemaphoreType.DMA((n,)),
        ],
        compiler_params=pltpu.CompilerParams(collective_id=0, has_side_effects=True),
        name="sum_over_devices",
    )(part)


def inverse(a):
    size = a.shape[0]
    lane = lax.broadcasted_iota(jnp.int32, (8, size), 1)
    sub = lax.broadcasted_iota(jnp.int32, (8, size), 0)
    wide_lane = lax.broadcasted_iota(jnp.int32, (size - 8, size), 1)

    def step(_, a):
        top, rest = a[:8], a[8:]
        cols = [jnp.broadcast_to(top[:, i : i + 1], top.shape) for i in range(8)]
        for i in range(8):
            col = cols[i]
            inv = 1.0 / col[i : i + 1]
            row = jnp.where(lane[:1] == i, inv, top[i : i + 1] * inv)
            top = jnp.where(sub == i, row, jnp.where(lane == i, 0.0, top) - col * row)
            for m in range(i + 1, 8):
                t = cols[m][i : i + 1] * inv
                cols[m] = jnp.where(sub == i, t, cols[m] - col * t)
        new = jnp.where(wide_lane < 8, 0.0, rest)
        for i in range(8):
            new = new - rest[:, i : i + 1] * top[i : i + 1]
        return pltpu.roll(jnp.concatenate([new, top], axis=0), size - 8, 1)

    return lax.fori_loop(0, size // 8, step, a)


def solve_kernel(both_ref, alpha_ref):
    width = both_ref.shape[1]
    full = 2 * width
    g11, g21 = both_ref[:width], both_ref[width:full]
    g12, g22 = both_ref[full : full + width], both_ref[full + width : 2 * full]
    p1 = jnp.concatenate([both_ref[2 * full : 2 * full + width], both_ref[3 * full : 3 * full + width]], axis=1)
    p2 = jnp.concatenate([both_ref[2 * full + width : 3 * full], both_ref[3 * full + width :]], axis=1)
    inv1 = inverse(g11)
    across = dot32(inv1, g12)
    part1 = dot32(inv1, p1)
    inv2 = inverse(g22 - dot32(g21, across))
    part2 = dot32(inv2, p2 - dot32(g21, part1))
    alpha_ref[width:] = part2
    alpha_ref[:width] = part1 - dot32(across, part2)


def solve(both, width):
    return pl.pallas_call(
        solve_kernel,
        out_shape=jax.ShapeDtypeStruct((width, width), jnp.float32),
        in_specs=[pl.BlockSpec(memory_space=pltpu.VMEM)],
        out_specs=pl.BlockSpec(memory_space=pltpu.VMEM),
        name="solve",
    )(both)


def shards(rhs, near_blocks, source_basis, target_basis, far_coupling, send_ids, far_list):
    rows, width = rhs.shape
    rank = source_basis.shape[1]
    leaves = rows // LEAF
    fanout = far_list.shape[1] // leaves
    senders = send_ids[0].reshape(-1)
    readers = far_list[0]
    source_leaf = source_basis.reshape(leaves, LEAF, rank)
    target_leaf = target_basis.reshape(leaves, LEAF, rank)
    solution = jnp.zeros_like(rhs)
    residual = rhs
    for step in range(ITERS):
        vb = residual.astype(jnp.bfloat16)
        ext = with_halo(vb, (("blk", 0),), HALO)
        coef = jnp.einsum(
            "lia,lis->las",
            source_leaf,
            vb.reshape(leaves, LEAF, width),
            preferred_element_type=jnp.float32,
        ).astype(jnp.bfloat16)
        outgoing = coef[senders]
        incoming = lax.all_to_all(
            outgoing, ("wide", "blk"), split_axis=0, concat_axis=0, tiled=True
        )
        near = near_apply(near_blocks, ext)
        picked = incoming[readers].reshape(leaves, fanout, rank, width)
        trans = jnp.einsum(
            "lfab,lfbs->las", far_coupling, picked, preferred_element_type=jnp.float32
        ).astype(jnp.bfloat16)
        far = jnp.einsum(
            "lia,las->lis", target_leaf, trans, preferred_element_type=jnp.float32
        ).reshape(rows, width)
        image = residual + near + far
        local_gram = jnp.einsum("rs,rt->st", image, image, precision=lax.Precision.HIGHEST)
        local_proj = jnp.einsum("rs,rt->st", image, residual, precision=lax.Precision.HIGHEST)
        half = width // 2
        part = jnp.concatenate(
            [local_gram[:, :half], local_gram[:, half:], local_proj[:, :half], local_proj[:, half:]], axis=0
        )
        n_blk = lax.axis_size("blk")
        both = sum_over_devices(part, lax.axis_size("wide") * n_blk, n_blk)
        alpha = solve(both, width)
        solution = solution + jnp.dot(residual, alpha, precision=lax.Precision.HIGHEST)
        residual = residual - jnp.dot(image, alpha, precision=lax.Precision.HIGHEST)
    return (solution, residual)


def solution(mesh):
    in_specs = (
        P(("wide", "blk"), None),
        P(("wide", "blk"), None),
        P(("wide", "blk"), None),
        P(("wide", "blk"), None),
        P(("wide", "blk"), None, None, None),
        P(("wide", "blk"), None, None),
        P(("wide", "blk"), None),
    )
    out_specs = (P(("wide", "blk"), None), P(("wide", "blk"), None))
    return jax.shard_map(shards, mesh=mesh, in_specs=in_specs, out_specs=out_specs, check_vma=False)
```

```python
import functools

import jax
import jax.numpy as jnp
from jax import lax
from jax.experimental import pallas as pl
from jax.experimental.pallas import tpu as pltpu
from jax.sharding import PartitionSpec as P

NEAR = 1024
HALO = 256
LEAF = 128
ITERS = 2


def sides(value, axis, width):
    count, length = lax.axis_size(axis), value.shape[0]
    up = [(i, (i + 1) % count) for i in range(count)]
    down = [(j, i) for i, j in up]
    return lax.ppermute(value[length - width :], axis, up), lax.ppermute(value[:width], axis, down)


def dot32(a, b):
    return jnp.dot(a, b, precision=lax.Precision.HIGHEST, preferred_element_type=jnp.float32)


def sum_kernel(n, n_blk, part_ref, out_ref, landed, total, sent, got, sent2, got2):
    me = lax.axis_index("wide") * n_blk + lax.axis_index("blk")
    chunk = part_ref.shape[0] // n

    def peer_of(d):
        return lax.rem(me + d, n)

    def place(p):
        return {"wide": p // n_blk, "blk": lax.rem(p, n_blk)}

    def rows(p):
        return pl.ds(pl.multiple_of(p * chunk, chunk), chunk)

    barrier = pltpu.get_barrier_semaphore()

    def greet(d, c):
        pl.semaphore_signal(barrier, inc=1, device_id=place(peer_of(d)), device_id_type=pl.DeviceIdType.MESH)
        return c

    lax.fori_loop(1, n, greet, 0)
    pl.semaphore_wait(barrier, n - 1)

    def scatter(d):
        p = peer_of(d)
        return pltpu.make_async_remote_copy(
            src_ref=part_ref.at[rows(p)],
            dst_ref=landed.at[rows(me)],
            send_sem=sent.at[d],
            recv_sem=got.at[me],
            device_id=place(p),
            device_id_type=pl.DeviceIdType.MESH,
        )

    def gather(d):
        p = peer_of(d)
        return pltpu.make_async_remote_copy(
            src_ref=total.at[rows(me)],
            dst_ref=total.at[rows(me)],
            send_sem=sent2.at[d],
            recv_sem=got2.at[me],
            device_id=place(p),
            device_id_type=pl.DeviceIdType.MESH,
        )

    def arrived(ref, sems, d):
        p = peer_of(d)
        return pltpu.make_async_remote_copy(
            src_ref=ref.at[rows(p)],
            dst_ref=ref.at[rows(p)],
            send_sem=sent.at[d],
            recv_sem=sems.at[p],
            device_id=place(p),
            device_id_type=pl.DeviceIdType.MESH,
        )

    def start1(d, c):
        scatter(d).start()
        return c

    lax.fori_loop(1, n, start1, 0)

    def add(d, acc):
        arrived(landed, got, d).wait_recv()
        return acc + landed[rows(peer_of(d))]

    acc = lax.fori_loop(1, n, add, part_ref[rows(me)])
    total[rows(me)] = acc

    def start2(d, c):
        gather(d).start()
        return c

    lax.fori_loop(1, n, start2, 0)

    def drain(d, c):
        scatter(d).wait_send()
        gather(d).wait_send()
        arrived(total, got2, d).wait_recv()
        return c

    lax.fori_loop(1, n, drain, 0)
    out_ref[...] = total[...]


def sum_over_devices(part, n, n_blk):
    return pl.pallas_call(
        functools.partial(sum_kernel, n, n_blk),
        out_shape=jax.ShapeDtypeStruct(part.shape, part.dtype),
        in_specs=[pl.BlockSpec(memory_space=pltpu.VMEM)],
        out_specs=pl.BlockSpec(memory_space=pltpu.VMEM),
        scratch_shapes=[
            pltpu.VMEM(part.shape, part.dtype),
            pltpu.VMEM(part.shape, part.dtype),
            pltpu.SemaphoreType.DMA((n,)),
            pltpu.SemaphoreType.DMA((n,)),
            pltpu.SemaphoreType.DMA((n,)),
            pltpu.SemaphoreType.DMA((n,)),
        ],
        compiler_params=pltpu.CompilerParams(collective_id=0, has_side_effects=True),
        name="sum_over_devices",
    )(part)


def inverse(a):
    size = a.shape[0]
    lane = lax.broadcasted_iota(jnp.int32, (8, size), 1)
    sub = lax.broadcasted_iota(jnp.int32, (8, size), 0)
    wide_lane = lax.broadcasted_iota(jnp.int32, (size - 8, size), 1)

    def step(_, a):
        top, rest = a[:8], a[8:]
        cols = [jnp.broadcast_to(top[:, i : i + 1], top.shape) for i in range(8)]
        for i in range(8):
            col = cols[i]
            inv = 1.0 / col[i : i + 1]
            row = jnp.where(lane[:1] == i, inv, top[i : i + 1] * inv)
            top = jnp.where(sub == i, row, jnp.where(lane == i, 0.0, top) - col * row)
            for m in range(i + 1, 8):
                t = cols[m][i : i + 1] * inv
                cols[m] = jnp.where(sub == i, t, cols[m] - col * t)
        new = jnp.where(wide_lane < 8, 0.0, rest)
        for i in range(8):
            new = new - rest[:, i : i + 1] * top[i : i + 1]
        return pltpu.roll(jnp.concatenate([new, top], axis=0), size - 8, 1)

    return lax.fori_loop(0, size // 8, step, a)


def solve_kernel(both_ref, alpha_ref):
    width = both_ref.shape[1]
    full = 2 * width
    g11, g21 = both_ref[:width], both_ref[width:full]
    g12, g22 = both_ref[full : full + width], both_ref[full + width : 2 * full]
    p1 = jnp.concatenate([both_ref[2 * full : 2 * full + width], both_ref[3 * full : 3 * full + width]], axis=1)
    p2 = jnp.concatenate([both_ref[2 * full + width : 3 * full], both_ref[3 * full + width :]], axis=1)
    inv1 = inverse(g11)
    across = dot32(inv1, g12)
    part1 = dot32(inv1, p1)
    inv2 = inverse(g22 - dot32(g21, across))
    part2 = dot32(inv2, p2 - dot32(g21, part1))
    alpha_ref[width:] = part2
    alpha_ref[:width] = part1 - dot32(across, part2)


def solve(both, width):
    return pl.pallas_call(
        solve_kernel,
        out_shape=jax.ShapeDtypeStruct((width, width), jnp.float32),
        in_specs=[pl.BlockSpec(memory_space=pltpu.VMEM)],
        out_specs=pl.BlockSpec(memory_space=pltpu.VMEM),
        name="solve",
    )(both)


TILE = 512
WHOLE = pl.BlockSpec(memory_space=pltpu.VMEM)


def split(x):
    high = x.astype(jnp.bfloat16)
    return high, (x - high.astype(jnp.float32)).astype(jnp.bfloat16)


def dot16(a, b):
    return jnp.dot(a, b, preferred_element_type=jnp.float32)


def tdot16(a, b):
    return lax.dot_general(a, b, (((0,), (0,)), ((), ())), preferred_element_type=jnp.float32)


def tiles(width):
    return pl.BlockSpec((TILE, width), lambda i: (i, 0))


def near_kernel(near_ref, vb_ref, before_ref, after_ref, res_ref, out_ref, ext):
    i = pl.program_id(0)
    halo, rows = before_ref.shape[0], vb_ref.shape[0]

    @pl.when(i == 0)
    def _():
        ext[:halo] = before_ref[...]
        ext[halo : halo + rows] = vb_ref[...]
        ext[halo + rows :] = after_ref[...]

    start = pl.multiple_of((i * TILE) // NEAR * NEAR, NEAR)
    out_ref[...] = res_ref[...] + dot16(near_ref[...], ext[pl.ds(start, near_ref.shape[1])])


def near_base(near_blocks, vb, before, after, residual):
    rows, width = residual.shape
    return pl.pallas_call(
        near_kernel,
        grid=(rows // TILE,),
        out_shape=jax.ShapeDtypeStruct(residual.shape, jnp.float32),
        in_specs=[tiles(near_blocks.shape[1]), WHOLE, WHOLE, WHOLE, tiles(width)],
        out_specs=tiles(width),
        scratch_shapes=[pltpu.VMEM((rows + 2 * HALO, width), jnp.bfloat16)],
        cost_estimate=pl.CostEstimate(
            flops=2 * rows * near_blocks.shape[1] * width, bytes_accessed=2 * near_blocks.size + 8 * residual.size, transcendentals=0
        ),
        name="near",
    )(near_blocks, vb, before, after, residual)


def image_kernel(fanout, list_ref, base_ref, res_ref, incoming_ref, coupling_ref, target_ref, image_ref, part_ref, cross):
    i = pl.program_id(0)
    width = base_ref.shape[1]
    half = width // 2
    leaves = TILE // LEAF

    @pl.when(i == 0)
    def _():
        part_ref[...] = jnp.zeros_like(part_ref)
        cross[...] = jnp.zeros_like(cross)

    for l in range(leaves):
        trans = 0.0
        for f in range(fanout):
            trans = trans + dot16(coupling_ref[l, f], incoming_ref[list_ref[(i * leaves + l) * fanout + f]])
        far = tdot16(target_ref[:, l * LEAF : (l + 1) * LEAF], trans.astype(jnp.bfloat16))
        image_ref[l * LEAF : (l + 1) * LEAF] = base_ref[l * LEAF : (l + 1) * LEAF] + far
    high, low = split(image_ref[...])
    res_high, res_low = split(res_ref[...])
    gram = tdot16(high, high)
    proj = tdot16(high, res_high) + tdot16(high, res_low) + tdot16(low, res_high)
    cross[...] += tdot16(high, low)
    part_ref[:width] += gram[:, :half]
    part_ref[width : 2 * width] += gram[:, half:]
    part_ref[2 * width : 3 * width] += proj[:, :half]
    part_ref[3 * width :] += proj[:, half:]

    @pl.when(i == pl.num_programs(0) - 1)
    def _():
        both = cross[...] + cross[...].T
        part_ref[:width] += both[:, :half]
        part_ref[width : 2 * width] += both[:, half:]


def image_and_sums(readers, base, residual, incoming, coupling, target_t):
    rows, width = residual.shape
    leaves, fanout, rank, _ = coupling.shape
    step = TILE // LEAF
    return pl.pallas_call(
        functools.partial(image_kernel, fanout),
        grid=(rows // TILE,),
        out_shape=(
            jax.ShapeDtypeStruct(residual.shape, jnp.float32),
            jax.ShapeDtypeStruct((4 * width, width // 2), jnp.float32),
        ),
        in_specs=[
            pl.BlockSpec(memory_space=pltpu.SMEM),
            tiles(width),
            tiles(width),
            WHOLE,
            pl.BlockSpec((step, fanout, rank, rank), lambda i: (i, 0, 0, 0)),
            pl.BlockSpec((rank, TILE), lambda i: (0, i)),
        ],
        out_specs=(tiles(width), pl.BlockSpec((4 * width, width // 2), lambda i: (0, 0))),
        scratch_shapes=[pltpu.VMEM((width, width), jnp.float32)],
        name="image",
    )(readers, base, residual, incoming, coupling, target_t)


def product(x, alpha_ref):
    high, low = split(x)
    a_high, a_low = split(alpha_ref[...])
    return dot16(high, a_high) + dot16(high, a_low) + dot16(low, a_high)


def update_kernel(res_ref, image_ref, alpha_ref, new_ref, vb_ref):
    new = res_ref[...] - product(image_ref[...], alpha_ref)
    new_ref[...] = new
    vb_ref[...] = new.astype(jnp.bfloat16)


def update(residual, image, alpha):
    rows, width = residual.shape
    return pl.pallas_call(
        update_kernel,
        grid=(rows // TILE,),
        out_shape=(
            jax.ShapeDtypeStruct(residual.shape, jnp.float32),
            jax.ShapeDtypeStruct(residual.shape, jnp.bfloat16),
        ),
        in_specs=[tiles(width), tiles(width), WHOLE],
        out_specs=(tiles(width), tiles(width)),
        name="update",
    )(residual, image, alpha)


def last_kernel(count, *refs):
    residuals, alphas, image_ref = refs[:count], refs[count : 2 * count], refs[2 * count]
    sol_ref, new_ref = refs[2 * count + 1 :]
    total = product(residuals[0][...], alphas[0])
    for res_ref, alpha_ref in zip(residuals[1:], alphas[1:]):
        total = total + product(res_ref[...], alpha_ref)
    sol_ref[...] = total
    new_ref[...] = residuals[-1][...] - product(image_ref[...], alphas[-1])


def last_update(residuals, alphas, image):
    rows, width = image.shape
    count = len(residuals)
    shape = jax.ShapeDtypeStruct(image.shape, jnp.float32)
    return pl.pallas_call(
        functools.partial(last_kernel, count),
        grid=(rows // TILE,),
        out_shape=(shape, shape),
        in_specs=[tiles(width)] * count + [WHOLE] * count + [tiles(width)],
        out_specs=(tiles(width), tiles(width)),
        name="last_update",
    )(*residuals, *alphas, image)


def shards(rhs, near_blocks, source_basis, target_basis, far_coupling, send_ids, far_list):
    rows, width = rhs.shape
    rank = source_basis.shape[1]
    leaves = rows // LEAF
    senders = send_ids[0].reshape(-1)
    readers = far_list[0]
    source_leaf = source_basis.reshape(leaves, LEAF, rank)
    target_t = target_basis.T
    n_blk = lax.axis_size("blk")
    n = lax.axis_size("wide") * n_blk
    residual = rhs
    vb = rhs.astype(jnp.bfloat16)
    residuals, alphas = [], []
    for step in range(ITERS):
        coef = jnp.einsum(
            "lia,lis->las",
            source_leaf,
            vb.reshape(leaves, LEAF, width),
            preferred_element_type=jnp.float32,
        ).astype(jnp.bfloat16)
        outgoing = coef[senders]
        incoming = lax.all_to_all(
            outgoing, ("wide", "blk"), split_axis=0, concat_axis=0, tiled=True
        )
        before, after = sides(vb, "blk", HALO)
        base = near_base(near_blocks, vb, before, after, residual)
        image, part = image_and_sums(readers, base, residual, incoming, far_coupling, target_t)
        both = sum_over_devices(part, n, n_blk)
        residuals.append(residual)
        alphas.append(solve(both, width))
        if step < ITERS - 1:
            residual, vb = update(residual, image, alphas[-1])
    return last_update(residuals, alphas, image)


def solution(mesh):
    in_specs = (
        P(("wide", "blk"), None),
        P(("wide", "blk"), None),
        P(("wide", "blk"), None),
        P(("wide", "blk"), None),
        P(("wide", "blk"), None, None, None),
        P(("wide", "blk"), None, None),
        P(("wide", "blk"), None),
    )
    out_specs = (P(("wide", "blk"), None), P(("wide", "blk"), None))
    return jax.shard_map(shards, mesh=mesh, in_specs=in_specs, out_specs=out_specs, check_vma=False)
```

```python
import functools

import jax
import jax.numpy as jnp
from jax import lax
from jax.experimental import pallas as pl
from jax.experimental.pallas import tpu as pltpu
from jax.sharding import PartitionSpec as P

NEAR = 1024
HALO = 256
LEAF = 128
ITERS = 2


def sides(value, axis, width):
    count, length = lax.axis_size(axis), value.shape[0]
    up = [(i, (i + 1) % count) for i in range(count)]
    down = [(j, i) for i, j in up]
    return lax.ppermute(value[length - width :], axis, up), lax.ppermute(value[:width], axis, down)


def dot32(a, b):
    return jnp.dot(a, b, precision=lax.Precision.HIGHEST, preferred_element_type=jnp.float32)


def sum_kernel(n, n_blk, part_ref, out_ref, other, mine, landed, total, pair_sem, sent, got, sent2, got2, sent3, got3):
    me = lax.axis_index("wide") * n_blk + lax.axis_index("blk")
    m = n // 2
    half = part_ref.shape[0] // 2
    chunk = half // m
    side = lax.rem(me, 2)
    idx = me // 2
    partner = me + 1 - 2 * side

    def peer_of(d):
        return lax.rem(idx + d, m)

    def place(p):
        return {"wide": p // n_blk, "blk": lax.rem(p, n_blk)}

    def rows(start, size):
        return pl.ds(pl.multiple_of(start, size), size)

    def send(src, dst, send_sem, recv_sem, device):
        return pltpu.make_async_remote_copy(
            src_ref=src,
            dst_ref=dst,
            send_sem=send_sem,
            recv_sem=recv_sem,
            device_id=place(device),
            device_id_type=pl.DeviceIdType.MESH,
        )

    barrier = pltpu.get_barrier_semaphore()

    def greet(d, c):
        pl.semaphore_signal(
            barrier, inc=1, device_id=place(2 * peer_of(d) + side), device_id_type=pl.DeviceIdType.MESH
        )
        return c

    pl.semaphore_signal(barrier, inc=1, device_id=place(partner), device_id_type=pl.DeviceIdType.MESH)
    lax.fori_loop(1, m, greet, 0)
    pl.semaphore_wait(barrier, m)

    pair = send(part_ref.at[rows((1 - side) * half, half)], other, pair_sem.at[0], pair_sem.at[1], partner)
    pair.start()
    pair.wait()
    mine[...] = part_ref[rows(side * half, half)] + other[...]

    def scatter(d):
        q = peer_of(d)
        return send(mine.at[rows(q * chunk, chunk)], landed.at[rows(idx * chunk, chunk)], sent.at[d], got.at[idx], 2 * q + side)

    def own(q):
        return total.at[rows(side * half + q * chunk, chunk)]

    def gather(d):
        return send(own(idx), own(idx), sent2.at[d], got2.at[idx], 2 * peer_of(d) + side)

    def forward(q):
        return send(own(q), own(q), sent3.at[q], got3.at[q], partner)

    def start1(d, c):
        scatter(d).start()
        return c

    lax.fori_loop(1, m, start1, 0)

    def add(d, acc):
        q = peer_of(d)
        slot = landed.at[rows(q * chunk, chunk)]
        send(slot, slot, sent.at[d], got.at[q], 2 * q + side).wait_recv()
        return acc + landed[rows(q * chunk, chunk)]

    total[rows(side * half + idx * chunk, chunk)] = lax.fori_loop(1, m, add, mine[rows(idx * chunk, chunk)])

    def start2(d, c):
        gather(d).start()
        return c

    lax.fori_loop(1, m, start2, 0)
    forward(idx).start()

    def relay(d, c):
        q = peer_of(d)
        send(own(q), own(q), sent2.at[d], got2.at[q], 2 * q + side).wait_recv()
        forward(q).start()
        return c

    lax.fori_loop(1, m, relay, 0)

    def drain(d, c):
        scatter(d).wait_send()
        gather(d).wait_send()
        return c

    lax.fori_loop(1, m, drain, 0)

    def finish(q, c):
        forward(q).wait_send()
        slot = total.at[rows((1 - side) * half + q * chunk, chunk)]
        send(slot, slot, sent3.at[q], got3.at[q], partner).wait_recv()
        return c

    lax.fori_loop(0, m, finish, 0)
    out_ref[...] = total[...]


def sum_over_devices(part, n, n_blk):
    half = (part.shape[0] // 2, part.shape[1])
    return pl.pallas_call(
        functools.partial(sum_kernel, n, n_blk),
        out_shape=jax.ShapeDtypeStruct(part.shape, part.dtype),
        in_specs=[pl.BlockSpec(memory_space=pltpu.VMEM)],
        out_specs=pl.BlockSpec(memory_space=pltpu.VMEM),
        scratch_shapes=[pltpu.VMEM(half, part.dtype)] * 3
        + [pltpu.VMEM(part.shape, part.dtype), pltpu.SemaphoreType.DMA((2,))]
        + [pltpu.SemaphoreType.DMA((n // 2,))] * 6,
        compiler_params=pltpu.CompilerParams(collective_id=0, has_side_effects=True),
        name="sum_over_devices",
    )(part)


def inverse(a):
    size = a.shape[0]
    lane = lax.broadcasted_iota(jnp.int32, (8, size), 1)
    sub = lax.broadcasted_iota(jnp.int32, (8, size), 0)
    wide_lane = lax.broadcasted_iota(jnp.int32, (size - 8, size), 1)

    def step(_, a):
        top, rest = a[:8], a[8:]
        cols = [jnp.broadcast_to(top[:, i : i + 1], top.shape) for i in range(8)]
        for i in range(8):
            col = cols[i]
            inv = 1.0 / col[i : i + 1]
            row = jnp.where(lane[:1] == i, inv, top[i : i + 1] * inv)
            top = jnp.where(sub == i, row, jnp.where(lane == i, 0.0, top) - col * row)
            for m in range(i + 1, 8):
                t = cols[m][i : i + 1] * inv
                cols[m] = jnp.where(sub == i, t, cols[m] - col * t)
        new = jnp.where(wide_lane < 8, 0.0, rest)
        for i in range(8):
            new = new - rest[:, i : i + 1] * top[i : i + 1]
        return pltpu.roll(jnp.concatenate([new, top], axis=0), size - 8, 1)

    return lax.fori_loop(0, size // 8, step, a)


def solve_kernel(both_ref, alpha_ref):
    width = both_ref.shape[1]
    full = 2 * width
    g11, g21 = both_ref[:width], both_ref[width:full]
    g12, g22 = both_ref[full : full + width], both_ref[full + width : 2 * full]
    p1 = jnp.concatenate([both_ref[2 * full : 2 * full + width], both_ref[3 * full : 3 * full + width]], axis=1)
    p2 = jnp.concatenate([both_ref[2 * full + width : 3 * full], both_ref[3 * full + width :]], axis=1)
    inv1 = inverse(g11)
    across = dot32(inv1, g12)
    part1 = dot32(inv1, p1)
    inv2 = inverse(g22 - dot32(g21, across))
    part2 = dot32(inv2, p2 - dot32(g21, part1))
    alpha_ref[width:] = part2
    alpha_ref[:width] = part1 - dot32(across, part2)


def solve(both, width):
    return pl.pallas_call(
        solve_kernel,
        out_shape=jax.ShapeDtypeStruct((width, width), jnp.float32),
        in_specs=[pl.BlockSpec(memory_space=pltpu.VMEM)],
        out_specs=pl.BlockSpec(memory_space=pltpu.VMEM),
        name="solve",
    )(both)


TILE = 512
WHOLE = pl.BlockSpec(memory_space=pltpu.VMEM)


def split(x):
    high = x.astype(jnp.bfloat16)
    return high, (x - high.astype(jnp.float32)).astype(jnp.bfloat16)


def dot16(a, b):
    return jnp.dot(a, b, preferred_element_type=jnp.float32)


def tdot16(a, b):
    return lax.dot_general(a, b, (((0,), (0,)), ((), ())), preferred_element_type=jnp.float32)


def tiles(width):
    return pl.BlockSpec((TILE, width), lambda i: (i, 0))


def near_kernel(near_ref, vb_ref, res_ref, out_ref, ext):
    i = pl.program_id(0)
    rows, width = vb_ref.shape

    @pl.when(i == 0)
    def _():
        ext[:HALO] = jnp.zeros((HALO, width), ext.dtype)
        ext[HALO : HALO + rows] = vb_ref[...]
        ext[HALO + rows :] = jnp.zeros((HALO, width), ext.dtype)

    start = pl.multiple_of((i * TILE) // NEAR * NEAR, NEAR)
    out_ref[...] = res_ref[...] + dot16(near_ref[...], ext[pl.ds(start, near_ref.shape[1])])


def near_base(near_blocks, vb, residual):
    rows, width = residual.shape
    return pl.pallas_call(
        near_kernel,
        grid=(rows // TILE,),
        out_shape=jax.ShapeDtypeStruct(residual.shape, jnp.float32),
        in_specs=[tiles(near_blocks.shape[1]), WHOLE, tiles(width)],
        out_specs=tiles(width),
        scratch_shapes=[pltpu.VMEM((rows + 2 * HALO, width), jnp.bfloat16)],
        cost_estimate=pl.CostEstimate(
            flops=2 * rows * near_blocks.shape[1] * width, bytes_accessed=2 * near_blocks.size + 8 * residual.size, transcendentals=0
        ),
        name="near",
    )(near_blocks, vb, residual)


def image_kernel(fanout, list_ref, base_ref, res_ref, incoming_ref, coupling_ref, target_ref, first_ref, last_ref, before_ref, after_ref, image_ref, part_ref, cross):
    i = pl.program_id(0)
    width = base_ref.shape[1]
    half = width // 2
    leaves = TILE // LEAF

    @pl.when(i == 0)
    def _():
        part_ref[...] = jnp.zeros_like(part_ref)
        cross[...] = jnp.zeros_like(cross)

    for l in range(leaves):
        trans = 0.0
        for f in range(fanout):
            trans = trans + dot16(coupling_ref[l, f], incoming_ref[list_ref[(i * leaves + l) * fanout + f]])
        far = tdot16(target_ref[:, l * LEAF : (l + 1) * LEAF], trans.astype(jnp.bfloat16))
        image_ref[l * LEAF : (l + 1) * LEAF] = base_ref[l * LEAF : (l + 1) * LEAF] + far

    @pl.when(i < NEAR // TILE)
    def _():
        image_ref[...] += dot16(first_ref[...], before_ref[...])

    @pl.when(i >= pl.num_programs(0) - NEAR // TILE)
    def _():
        image_ref[...] += dot16(last_ref[...], after_ref[...])

    high, low = split(image_ref[...])
    res_high, res_low = split(res_ref[...])
    gram = tdot16(high, high)
    proj = tdot16(high, res_high) + tdot16(high, res_low) + tdot16(low, res_high)
    cross[...] += tdot16(high, low)
    part_ref[:width] += gram[:, :half]
    part_ref[width : 2 * width] += gram[:, half:]
    part_ref[2 * width : 3 * width] += proj[:, :half]
    part_ref[3 * width :] += proj[:, half:]

    @pl.when(i == pl.num_programs(0) - 1)
    def _():
        both = cross[...] + cross[...].T
        part_ref[:width] += both[:, :half]
        part_ref[width : 2 * width] += both[:, half:]


def image_and_sums(readers, base, residual, incoming, coupling, target_t, near_blocks, before, after):
    rows, width = residual.shape
    leaves, fanout, rank, _ = coupling.shape
    step = TILE // LEAF
    edge, steps = NEAR // TILE, rows // TILE
    last_column = near_blocks.shape[1] // HALO - 1
    return pl.pallas_call(
        functools.partial(image_kernel, fanout),
        grid=(rows // TILE,),
        out_shape=(
            jax.ShapeDtypeStruct(residual.shape, jnp.float32),
            jax.ShapeDtypeStruct((4 * width, width // 2), jnp.float32),
        ),
        in_specs=[
            pl.BlockSpec(memory_space=pltpu.SMEM),
            tiles(width),
            tiles(width),
            WHOLE,
            pl.BlockSpec((step, fanout, rank, rank), lambda i: (i, 0, 0, 0)),
            pl.BlockSpec((rank, TILE), lambda i: (0, i)),
            pl.BlockSpec((TILE, HALO), lambda i: (jnp.minimum(i, edge - 1), 0)),
            pl.BlockSpec((TILE, HALO), lambda i: (jnp.maximum(i, steps - edge), last_column)),
            WHOLE,
            WHOLE,
        ],
        out_specs=(tiles(width), pl.BlockSpec((4 * width, width // 2), lambda i: (0, 0))),
        scratch_shapes=[pltpu.VMEM((width, width), jnp.float32)],
        name="image",
    )(readers, base, residual, incoming, coupling, target_t, near_blocks, near_blocks, before, after)


def product(x, alpha_ref):
    high, low = split(x)
    a_high, a_low = split(alpha_ref[...])
    return dot16(high, a_high) + dot16(high, a_low) + dot16(low, a_high)


def update_kernel(res_ref, image_ref, alpha_ref, new_ref, vb_ref):
    new = res_ref[...] - product(image_ref[...], alpha_ref)
    new_ref[...] = new
    vb_ref[...] = new.astype(jnp.bfloat16)


def update(residual, image, alpha):
    rows, width = residual.shape
    return pl.pallas_call(
        update_kernel,
        grid=(rows // TILE,),
        out_shape=(
            jax.ShapeDtypeStruct(residual.shape, jnp.float32),
            jax.ShapeDtypeStruct(residual.shape, jnp.bfloat16),
        ),
        in_specs=[tiles(width), tiles(width), WHOLE],
        out_specs=(tiles(width), tiles(width)),
        name="update",
    )(residual, image, alpha)


def last_kernel(count, *refs):
    residuals, alphas, image_ref = refs[:count], refs[count : 2 * count], refs[2 * count]
    sol_ref, new_ref = refs[2 * count + 1 :]
    total = product(residuals[0][...], alphas[0])
    for res_ref, alpha_ref in zip(residuals[1:], alphas[1:]):
        total = total + product(res_ref[...], alpha_ref)
    sol_ref[...] = total
    new_ref[...] = residuals[-1][...] - product(image_ref[...], alphas[-1])


def last_update(residuals, alphas, image):
    rows, width = image.shape
    count = len(residuals)
    shape = jax.ShapeDtypeStruct(image.shape, jnp.float32)
    return pl.pallas_call(
        functools.partial(last_kernel, count),
        grid=(rows // TILE,),
        out_shape=(shape, shape),
        in_specs=[tiles(width)] * count + [WHOLE] * count + [tiles(width)],
        out_specs=(tiles(width), tiles(width)),
        name="last_update",
    )(*residuals, *alphas, image)


def shards(rhs, near_blocks, source_basis, target_basis, far_coupling, send_ids, far_list):
    rows, width = rhs.shape
    rank = source_basis.shape[1]
    leaves = rows // LEAF
    senders = send_ids[0].reshape(-1)
    readers = far_list[0]
    source_leaf = source_basis.reshape(leaves, LEAF, rank)
    target_t = target_basis.T
    n_blk = lax.axis_size("blk")
    n = lax.axis_size("wide") * n_blk
    residual = rhs
    vb = rhs.astype(jnp.bfloat16)
    residuals, alphas = [], []
    for step in range(ITERS):
        coef = jnp.einsum(
            "lia,lis->las",
            source_leaf,
            vb.reshape(leaves, LEAF, width),
            preferred_element_type=jnp.float32,
        ).astype(jnp.bfloat16)
        outgoing = coef[senders]
        incoming = lax.all_to_all(
            outgoing, ("wide", "blk"), split_axis=0, concat_axis=0, tiled=True
        )
        before, after = sides(vb, "blk", HALO)
        base = near_base(near_blocks, vb, residual)
        image, part = image_and_sums(
            readers, base, residual, incoming, far_coupling, target_t, near_blocks, before, after
        )
        both = sum_over_devices(part, n, n_blk)
        residuals.append(residual)
        alphas.append(solve(both, width))
        if step < ITERS - 1:
            residual, vb = update(residual, image, alphas[-1])
    return last_update(residuals, alphas, image)


def solution(mesh):
    in_specs = (
        P(("wide", "blk"), None),
        P(("wide", "blk"), None),
        P(("wide", "blk"), None),
        P(("wide", "blk"), None),
        P(("wide", "blk"), None, None, None),
        P(("wide", "blk"), None, None),
        P(("wide", "blk"), None),
    )
    out_specs = (P(("wide", "blk"), None), P(("wide", "blk"), None))
    return jax.shard_map(shards, mesh=mesh, in_specs=in_specs, out_specs=out_specs, check_vma=False)
```

```python
import functools

import jax
import jax.numpy as jnp
from jax import lax
from jax.experimental import pallas as pl
from jax.experimental.pallas import tpu as pltpu
from jax.sharding import PartitionSpec as P

NEAR = 1024
HALO = 256
LEAF = 128
ITERS = 2


def sides(value, axis, width):
    count, length = lax.axis_size(axis), value.shape[0]
    up = [(i, (i + 1) % count) for i in range(count)]
    down = [(j, i) for i, j in up]
    return lax.ppermute(value[length - width :], axis, up), lax.ppermute(value[:width], axis, down)


def dot32(a, b):
    return jnp.dot(a, b, precision=lax.Precision.HIGHEST, preferred_element_type=jnp.float32)


def sum_kernel(n, n_blk, part_ref, out_ref, other, mine, landed, total, pair_sem, sent, got, sent2, got2, sent3, got3):
    me = lax.axis_index("wide") * n_blk + lax.axis_index("blk")
    m = n // 2
    half = part_ref.shape[0] // 2
    chunk = half // m
    side = lax.rem(me, 2)
    idx = me // 2
    partner = me + 1 - 2 * side

    def peer_of(d):
        return lax.rem(idx + d, m)

    def place(p):
        return {"wide": p // n_blk, "blk": lax.rem(p, n_blk)}

    def rows(start, size):
        return pl.ds(pl.multiple_of(start, size), size)

    def send(src, dst, send_sem, recv_sem, device):
        return pltpu.make_async_remote_copy(
            src_ref=src,
            dst_ref=dst,
            send_sem=send_sem,
            recv_sem=recv_sem,
            device_id=place(device),
            device_id_type=pl.DeviceIdType.MESH,
        )

    barrier = pltpu.get_barrier_semaphore()

    def greet(d, c):
        pl.semaphore_signal(
            barrier, inc=1, device_id=place(2 * peer_of(d) + side), device_id_type=pl.DeviceIdType.MESH
        )
        return c

    pl.semaphore_signal(barrier, inc=1, device_id=place(partner), device_id_type=pl.DeviceIdType.MESH)
    lax.fori_loop(1, m, greet, 0)
    pl.semaphore_wait(barrier, m)

    pair = send(part_ref.at[rows((1 - side) * half, half)], other, pair_sem.at[0], pair_sem.at[1], partner)
    pair.start()
    pair.wait()
    mine[...] = part_ref[rows(side * half, half)] + other[...]

    def scatter(d):
        q = peer_of(d)
        return send(mine.at[rows(q * chunk, chunk)], landed.at[rows(idx * chunk, chunk)], sent.at[d], got.at[idx], 2 * q + side)

    def own(q):
        return total.at[rows(side * half + q * chunk, chunk)]

    def gather(d):
        return send(own(idx), own(idx), sent2.at[d], got2.at[idx], 2 * peer_of(d) + side)

    def forward(q):
        return send(own(q), own(q), sent3.at[q], got3.at[q], partner)

    def start1(d, c):
        scatter(d).start()
        return c

    lax.fori_loop(1, m, start1, 0)

    def add(d, acc):
        q = peer_of(d)
        slot = landed.at[rows(q * chunk, chunk)]
        send(slot, slot, sent.at[d], got.at[q], 2 * q + side).wait_recv()
        return acc + landed[rows(q * chunk, chunk)]

    total[rows(side * half + idx * chunk, chunk)] = lax.fori_loop(1, m, add, mine[rows(idx * chunk, chunk)])

    def start2(d, c):
        gather(d).start()
        return c

    lax.fori_loop(1, m, start2, 0)
    forward(idx).start()

    def relay(d, c):
        q = peer_of(d)
        send(own(q), own(q), sent2.at[d], got2.at[q], 2 * q + side).wait_recv()
        forward(q).start()
        return c

    lax.fori_loop(1, m, relay, 0)

    def drain(d, c):
        scatter(d).wait_send()
        gather(d).wait_send()
        return c

    lax.fori_loop(1, m, drain, 0)

    def finish(q, c):
        forward(q).wait_send()
        slot = total.at[rows((1 - side) * half + q * chunk, chunk)]
        send(slot, slot, sent3.at[q], got3.at[q], partner).wait_recv()
        return c

    lax.fori_loop(0, m, finish, 0)
    out_ref[...] = total[...]


def sum_over_devices(part, n, n_blk):
    half = (part.shape[0] // 2, part.shape[1])
    return pl.pallas_call(
        functools.partial(sum_kernel, n, n_blk),
        out_shape=jax.ShapeDtypeStruct(part.shape, part.dtype),
        in_specs=[pl.BlockSpec(memory_space=pltpu.VMEM)],
        out_specs=pl.BlockSpec(memory_space=pltpu.VMEM),
        scratch_shapes=[pltpu.VMEM(half, part.dtype)] * 3
        + [pltpu.VMEM(part.shape, part.dtype), pltpu.SemaphoreType.DMA((2,))]
        + [pltpu.SemaphoreType.DMA((n // 2,))] * 6,
        compiler_params=pltpu.CompilerParams(collective_id=0, has_side_effects=True),
        name="sum_over_devices",
    )(part)


def inverse(a):
    size = a.shape[0]
    lane = lax.broadcasted_iota(jnp.int32, (8, size), 1)
    sub = lax.broadcasted_iota(jnp.int32, (8, size), 0)
    wide_lane = lax.broadcasted_iota(jnp.int32, (size - 8, size), 1)

    def step(_, a):
        top, rest = a[:8], a[8:]
        cols = [jnp.broadcast_to(top[:, i : i + 1], top.shape) for i in range(8)]
        for i in range(8):
            col = cols[i]
            inv = 1.0 / col[i : i + 1]
            row = jnp.where(lane[:1] == i, inv, top[i : i + 1] * inv)
            top = jnp.where(sub == i, row, jnp.where(lane == i, 0.0, top) - col * row)
            for m in range(i + 1, 8):
                t = cols[m][i : i + 1] * inv
                cols[m] = jnp.where(sub == i, t, cols[m] - col * t)
        new = jnp.where(wide_lane < 8, 0.0, rest)
        for i in range(8):
            new = new - rest[:, i : i + 1] * top[i : i + 1]
        return pltpu.roll(jnp.concatenate([new, top], axis=0), size - 8, 1)

    return lax.fori_loop(0, size // 8, step, a)


def solve_kernel(both_ref, alpha_ref):
    width = both_ref.shape[1]
    full = 2 * width
    g11, g21 = both_ref[:width], both_ref[width:full]
    g12, g22 = both_ref[full : full + width], both_ref[full + width : 2 * full]
    p1 = jnp.concatenate([both_ref[2 * full : 2 * full + width], both_ref[3 * full : 3 * full + width]], axis=1)
    p2 = jnp.concatenate([both_ref[2 * full + width : 3 * full], both_ref[3 * full + width :]], axis=1)
    inv1 = inverse(g11)
    across = dot32(inv1, g12)
    part1 = dot32(inv1, p1)
    inv2 = inverse(g22 - dot32(g21, across))
    part2 = dot32(inv2, p2 - dot32(g21, part1))
    alpha_ref[width:] = part2
    alpha_ref[:width] = part1 - dot32(across, part2)


def solve(both, width):
    return pl.pallas_call(
        solve_kernel,
        out_shape=jax.ShapeDtypeStruct((width, width), jnp.float32),
        in_specs=[pl.BlockSpec(memory_space=pltpu.VMEM)],
        out_specs=pl.BlockSpec(memory_space=pltpu.VMEM),
        name="solve",
    )(both)


TILE = 512
WHOLE = pl.BlockSpec(memory_space=pltpu.VMEM)


def split(x):
    high = x.astype(jnp.bfloat16)
    return high, (x - high.astype(jnp.float32)).astype(jnp.bfloat16)


def dot16(a, b):
    return jnp.dot(a, b, preferred_element_type=jnp.float32)


def tdot16(a, b):
    return lax.dot_general(a, b, (((0,), (0,)), ((), ())), preferred_element_type=jnp.float32)


def tiles(width):
    return pl.BlockSpec((TILE, width), lambda i: (i, 0))


def near_kernel(near_ref, vb_ref, res_ref, out_ref, ext):
    i = pl.program_id(0)
    rows, width = vb_ref.shape

    @pl.when(i == 0)
    def _():
        ext[:HALO] = jnp.zeros((HALO, width), ext.dtype)
        ext[HALO : HALO + rows] = vb_ref[...]
        ext[HALO + rows :] = jnp.zeros((HALO, width), ext.dtype)

    start = pl.multiple_of((i * TILE) // NEAR * NEAR, NEAR)
    out_ref[...] = res_ref[...] + dot16(near_ref[...], ext[pl.ds(start, near_ref.shape[1])])


def near_base(near_blocks, vb, residual):
    rows, width = residual.shape
    return pl.pallas_call(
        near_kernel,
        grid=(rows // TILE,),
        out_shape=jax.ShapeDtypeStruct(residual.shape, jnp.float32),
        in_specs=[tiles(near_blocks.shape[1]), WHOLE, tiles(width)],
        out_specs=tiles(width),
        scratch_shapes=[pltpu.VMEM((rows + 2 * HALO, width), jnp.bfloat16)],
        cost_estimate=pl.CostEstimate(
            flops=2 * rows * near_blocks.shape[1] * width, bytes_accessed=2 * near_blocks.size + 8 * residual.size, transcendentals=0
        ),
        name="near",
    )(near_blocks, vb, residual)


def image_kernel(fanout, list_ref, base_ref, res_ref, incoming_ref, coupling_ref, target_ref, first_ref, last_ref, before_ref, after_ref, image_ref, part_ref, cross):
    i = pl.program_id(0)
    width = base_ref.shape[1]
    half = width // 2
    leaves = TILE // LEAF

    @pl.when(i == 0)
    def _():
        part_ref[...] = jnp.zeros_like(part_ref)
        cross[...] = jnp.zeros_like(cross)

    for l in range(leaves):
        trans = 0.0
        for f in range(fanout):
            trans = trans + dot16(coupling_ref[l, f], incoming_ref[list_ref[(i * leaves + l) * fanout + f]])
        far = tdot16(target_ref[:, l * LEAF : (l + 1) * LEAF], trans.astype(jnp.bfloat16))
        image_ref[l * LEAF : (l + 1) * LEAF] = base_ref[l * LEAF : (l + 1) * LEAF] + far

    @pl.when(i < NEAR // TILE)
    def _():
        image_ref[...] += dot16(first_ref[...], before_ref[...])

    @pl.when(i >= pl.num_programs(0) - NEAR // TILE)
    def _():
        image_ref[...] += dot16(last_ref[...], after_ref[...])

    high, low = split(image_ref[...])
    res_high, res_low = split(res_ref[...])
    sums = tdot16(high, jnp.concatenate([high, low, res_high, res_low], axis=1))
    gram = sums[:, :width]
    proj = sums[:, 2 * width : 3 * width] + sums[:, 3 * width :] + tdot16(low, res_high)
    cross[...] += sums[:, width : 2 * width]
    part_ref[:width] += gram[:, :half]
    part_ref[width : 2 * width] += gram[:, half:]
    part_ref[2 * width : 3 * width] += proj[:, :half]
    part_ref[3 * width :] += proj[:, half:]

    @pl.when(i == pl.num_programs(0) - 1)
    def _():
        both = cross[...] + cross[...].T
        part_ref[:width] += both[:, :half]
        part_ref[width : 2 * width] += both[:, half:]


def image_and_sums(readers, base, residual, incoming, coupling, target_t, near_blocks, before, after):
    rows, width = residual.shape
    leaves, fanout, rank, _ = coupling.shape
    step = TILE // LEAF
    edge, steps = NEAR // TILE, rows // TILE
    last_column = near_blocks.shape[1] // HALO - 1
    return pl.pallas_call(
        functools.partial(image_kernel, fanout),
        grid=(rows // TILE,),
        out_shape=(
            jax.ShapeDtypeStruct(residual.shape, jnp.float32),
            jax.ShapeDtypeStruct((4 * width, width // 2), jnp.float32),
        ),
        in_specs=[
            pl.BlockSpec(memory_space=pltpu.SMEM),
            tiles(width),
            tiles(width),
            WHOLE,
            pl.BlockSpec((step, fanout, rank, rank), lambda i: (i, 0, 0, 0)),
            pl.BlockSpec((rank, TILE), lambda i: (0, i)),
            pl.BlockSpec((TILE, HALO), lambda i: (jnp.minimum(i, edge - 1), 0)),
            pl.BlockSpec((TILE, HALO), lambda i: (jnp.maximum(i, steps - edge), last_column)),
            WHOLE,
            WHOLE,
        ],
        out_specs=(tiles(width), pl.BlockSpec((4 * width, width // 2), lambda i: (0, 0))),
        scratch_shapes=[pltpu.VMEM((width, width), jnp.float32)],
        name="image",
    )(readers, base, residual, incoming, coupling, target_t, near_blocks, near_blocks, before, after)


def product(x, alpha_ref):
    high, low = split(x)
    a_high, a_low = split(alpha_ref[...])
    return dot16(high, a_high) + dot16(high, a_low) + dot16(low, a_high)


def update_kernel(res_ref, image_ref, alpha_ref, source_ref, new_ref, vb_ref, coef_ref):
    new = res_ref[...] - product(image_ref[...], alpha_ref)
    new_ref[...] = new
    vb = new.astype(jnp.bfloat16)
    vb_ref[...] = vb
    for l in range(TILE // LEAF):
        leaf = slice(l * LEAF, (l + 1) * LEAF)
        coef_ref[l] = dot16(source_ref[:, leaf], vb[leaf]).astype(jnp.bfloat16)


def update(residual, image, alpha, source_t):
    rows, width = residual.shape
    rank, step = source_t.shape[0], TILE // LEAF
    return pl.pallas_call(
        update_kernel,
        grid=(rows // TILE,),
        out_shape=(
            jax.ShapeDtypeStruct(residual.shape, jnp.float32),
            jax.ShapeDtypeStruct(residual.shape, jnp.bfloat16),
            jax.ShapeDtypeStruct((rows // LEAF, rank, width), jnp.bfloat16),
        ),
        in_specs=[tiles(width), tiles(width), WHOLE, pl.BlockSpec((rank, TILE), lambda i: (0, i))],
        out_specs=(tiles(width), tiles(width), pl.BlockSpec((step, rank, width), lambda i: (i, 0, 0))),
        name="update",
    )(residual, image, alpha, source_t)


def last_kernel(count, *refs):
    residuals, alphas, image_ref = refs[:count], refs[count : 2 * count], refs[2 * count]
    sol_ref, new_ref = refs[2 * count + 1 :]
    total = product(residuals[0][...], alphas[0])
    for res_ref, alpha_ref in zip(residuals[1:], alphas[1:]):
        total = total + product(res_ref[...], alpha_ref)
    sol_ref[...] = total
    new_ref[...] = residuals[-1][...] - product(image_ref[...], alphas[-1])


def last_update(residuals, alphas, image):
    rows, width = image.shape
    count = len(residuals)
    shape = jax.ShapeDtypeStruct(image.shape, jnp.float32)
    return pl.pallas_call(
        functools.partial(last_kernel, count),
        grid=(rows // TILE,),
        out_shape=(shape, shape),
        in_specs=[tiles(width)] * count + [WHOLE] * count + [tiles(width)],
        out_specs=(tiles(width), tiles(width)),
        name="last_update",
    )(*residuals, *alphas, image)


def shards(rhs, near_blocks, source_basis, target_basis, far_coupling, send_ids, far_list):
    rows, width = rhs.shape
    rank = source_basis.shape[1]
    leaves = rows // LEAF
    senders = send_ids[0].reshape(-1)
    readers = far_list[0]
    source_leaf = source_basis.reshape(leaves, LEAF, rank)
    target_t = target_basis.T
    n_blk = lax.axis_size("blk")
    n = lax.axis_size("wide") * n_blk
    residual = rhs
    vb = rhs.astype(jnp.bfloat16)
    coef = jnp.einsum(
        "lia,lis->las", source_leaf, vb.reshape(leaves, LEAF, width), preferred_element_type=jnp.float32
    ).astype(jnp.bfloat16)
    residuals, alphas = [], []
    for step in range(ITERS):
        outgoing = coef[senders]
        incoming = lax.all_to_all(
            outgoing, ("wide", "blk"), split_axis=0, concat_axis=0, tiled=True
        )
        before, after = sides(vb, "blk", HALO)
        base = near_base(near_blocks, vb, residual)
        image, part = image_and_sums(
            readers, base, residual, incoming, far_coupling, target_t, near_blocks, before, after
        )
        both = sum_over_devices(part, n, n_blk)
        residuals.append(residual)
        alphas.append(solve(both, width))
        if step < ITERS - 1:
            residual, vb, coef = update(residual, image, alphas[-1], source_basis.T)
    return last_update(residuals, alphas, image)


def solution(mesh):
    in_specs = (
        P(("wide", "blk"), None),
        P(("wide", "blk"), None),
        P(("wide", "blk"), None),
        P(("wide", "blk"), None),
        P(("wide", "blk"), None, None, None),
        P(("wide", "blk"), None, None),
        P(("wide", "blk"), None),
    )
    out_specs = (P(("wide", "blk"), None), P(("wide", "blk"), None))
    return jax.shard_map(shards, mesh=mesh, in_specs=in_specs, out_specs=out_specs, check_vma=False)
```

```python
import functools

import jax
import jax.numpy as jnp
from jax import lax
from jax.experimental import pallas as pl
from jax.experimental.pallas import tpu as pltpu
from jax.sharding import PartitionSpec as P

NEAR = 1024
HALO = 256
LEAF = 128
ITERS = 2


def sides(value, axis, width):
    count, length = lax.axis_size(axis), value.shape[0]
    up = [(i, (i + 1) % count) for i in range(count)]
    down = [(j, i) for i, j in up]
    return lax.ppermute(value[length - width :], axis, up), lax.ppermute(value[:width], axis, down)


def dot32(a, b):
    return jnp.dot(a, b, precision=lax.Precision.HIGHEST, preferred_element_type=jnp.float32)


def sum_kernel(n, n_blk, part_ref, out_ref, other, mine, landed, total, pair_sem, sent, got, sent2, got2, sent3, got3):
    me = lax.axis_index("wide") * n_blk + lax.axis_index("blk")
    m = n // 2
    half = part_ref.shape[0] // 2
    chunk = half // m
    side = lax.rem(me, 2)
    idx = me // 2
    partner = me + 1 - 2 * side

    def peer_of(d):
        return lax.rem(idx + d, m)

    def place(p):
        return {"wide": p // n_blk, "blk": lax.rem(p, n_blk)}

    def rows(start, size):
        return pl.ds(pl.multiple_of(start, size), size)

    def send(src, dst, send_sem, recv_sem, device):
        return pltpu.make_async_remote_copy(
            src_ref=src,
            dst_ref=dst,
            send_sem=send_sem,
            recv_sem=recv_sem,
            device_id=place(device),
            device_id_type=pl.DeviceIdType.MESH,
        )

    barrier = pltpu.get_barrier_semaphore()

    def greet(d, c):
        pl.semaphore_signal(
            barrier, inc=1, device_id=place(2 * peer_of(d) + side), device_id_type=pl.DeviceIdType.MESH
        )
        return c

    pl.semaphore_signal(barrier, inc=1, device_id=place(partner), device_id_type=pl.DeviceIdType.MESH)
    lax.fori_loop(1, m, greet, 0)
    pl.semaphore_wait(barrier, m)

    pair = send(part_ref.at[rows((1 - side) * half, half)], other, pair_sem.at[0], pair_sem.at[1], partner)
    pair.start()
    pair.wait()
    mine[...] = part_ref[rows(side * half, half)] + other[...]

    def scatter(d):
        q = peer_of(d)
        return send(mine.at[rows(q * chunk, chunk)], landed.at[rows(idx * chunk, chunk)], sent.at[d], got.at[idx], 2 * q + side)

    def own(q):
        return total.at[rows(side * half + q * chunk, chunk)]

    def gather(d):
        return send(own(idx), own(idx), sent2.at[d], got2.at[idx], 2 * peer_of(d) + side)

    def forward(q):
        return send(own(q), own(q), sent3.at[q], got3.at[q], partner)

    def start1(d, c):
        scatter(d).start()
        return c

    lax.fori_loop(1, m, start1, 0)

    def add(d, acc):
        q = peer_of(d)
        slot = landed.at[rows(q * chunk, chunk)]
        send(slot, slot, sent.at[d], got.at[q], 2 * q + side).wait_recv()
        return acc + landed[rows(q * chunk, chunk)]

    total[rows(side * half + idx * chunk, chunk)] = lax.fori_loop(1, m, add, mine[rows(idx * chunk, chunk)])

    def start2(d, c):
        gather(d).start()
        return c

    lax.fori_loop(1, m, start2, 0)
    forward(idx).start()

    def relay(d, c):
        q = peer_of(d)
        send(own(q), own(q), sent2.at[d], got2.at[q], 2 * q + side).wait_recv()
        forward(q).start()
        return c

    lax.fori_loop(1, m, relay, 0)

    def drain(d, c):
        scatter(d).wait_send()
        gather(d).wait_send()
        return c

    lax.fori_loop(1, m, drain, 0)

    def finish(q, c):
        forward(q).wait_send()
        slot = total.at[rows((1 - side) * half + q * chunk, chunk)]
        send(slot, slot, sent3.at[q], got3.at[q], partner).wait_recv()
        return c

    lax.fori_loop(0, m, finish, 0)
    out_ref[...] = total[...]


def sum_over_devices(part, n, n_blk):
    half = (part.shape[0] // 2, part.shape[1])
    return pl.pallas_call(
        functools.partial(sum_kernel, n, n_blk),
        out_shape=jax.ShapeDtypeStruct(part.shape, part.dtype),
        in_specs=[pl.BlockSpec(memory_space=pltpu.VMEM)],
        out_specs=pl.BlockSpec(memory_space=pltpu.VMEM),
        scratch_shapes=[pltpu.VMEM(half, part.dtype)] * 3
        + [pltpu.VMEM(part.shape, part.dtype), pltpu.SemaphoreType.DMA((2,))]
        + [pltpu.SemaphoreType.DMA((n // 2,))] * 6,
        compiler_params=pltpu.CompilerParams(collective_id=0, has_side_effects=True),
        name="sum_over_devices",
    )(part)


def inverse(a):
    size = a.shape[0]
    lane = lax.broadcasted_iota(jnp.int32, (8, size), 1)
    sub = lax.broadcasted_iota(jnp.int32, (8, size), 0)
    wide_lane = lax.broadcasted_iota(jnp.int32, (size - 8, size), 1)

    def step(_, a):
        top, rest = a[:8], a[8:]
        cols = [jnp.broadcast_to(top[:, i : i + 1], top.shape) for i in range(8)]
        for i in range(8):
            col = cols[i]
            inv = 1.0 / col[i : i + 1]
            row = jnp.where(lane[:1] == i, inv, top[i : i + 1] * inv)
            top = jnp.where(sub == i, row, jnp.where(lane == i, 0.0, top) - col * row)
            for m in range(i + 1, 8):
                t = cols[m][i : i + 1] * inv
                cols[m] = jnp.where(sub == i, t, cols[m] - col * t)
        new = jnp.where(wide_lane < 8, 0.0, rest)
        for i in range(8):
            new = new - rest[:, i : i + 1] * top[i : i + 1]
        return pltpu.roll(jnp.concatenate([new, top], axis=0), size - 8, 1)

    return lax.fori_loop(0, size // 8, step, a)


def solve_kernel(both_ref, alpha_ref):
    width = both_ref.shape[1]
    full = 2 * width
    g11, g21 = both_ref[:width], both_ref[width:full]
    g12, g22 = both_ref[full : full + width], both_ref[full + width : 2 * full]
    p1 = jnp.concatenate([both_ref[2 * full : 2 * full + width], both_ref[3 * full : 3 * full + width]], axis=1)
    p2 = jnp.concatenate([both_ref[2 * full + width : 3 * full], both_ref[3 * full + width :]], axis=1)
    inv1 = inverse(g11)
    across = dot32(inv1, g12)
    part1 = dot32(inv1, p1)
    inv2 = inverse(g22 - dot32(g21, across))
    part2 = dot32(inv2, p2 - dot32(g21, part1))
    alpha_ref[width:] = part2
    alpha_ref[:width] = part1 - dot32(across, part2)


def solve(both, width):
    return pl.pallas_call(
        solve_kernel,
        out_shape=jax.ShapeDtypeStruct((width, width), jnp.float32),
        in_specs=[pl.BlockSpec(memory_space=pltpu.VMEM)],
        out_specs=pl.BlockSpec(memory_space=pltpu.VMEM),
        name="solve",
    )(both)


TILE = 512
IMAGE_TILE = 1024
WHOLE = pl.BlockSpec(memory_space=pltpu.VMEM)


def split(x):
    high = x.astype(jnp.bfloat16)
    return high, (x - high.astype(jnp.float32)).astype(jnp.bfloat16)


def dot16(a, b):
    return jnp.dot(a, b, preferred_element_type=jnp.float32)


def tdot16(a, b):
    return lax.dot_general(a, b, (((0,), (0,)), ((), ())), preferred_element_type=jnp.float32)


def tiles(width, tile=TILE):
    return pl.BlockSpec((tile, width), lambda i: (i, 0))


def near_kernel(near_ref, vb_ref, res_ref, out_ref, ext):
    i = pl.program_id(0)
    rows, width = vb_ref.shape

    @pl.when(i == 0)
    def _():
        ext[:HALO] = jnp.zeros((HALO, width), ext.dtype)
        ext[HALO : HALO + rows] = vb_ref[...]
        ext[HALO + rows :] = jnp.zeros((HALO, width), ext.dtype)

    start = pl.multiple_of((i * TILE) // NEAR * NEAR, NEAR)
    out_ref[...] = res_ref[...] + dot16(near_ref[...], ext[pl.ds(start, near_ref.shape[1])])


def near_base(near_blocks, vb, residual):
    rows, width = residual.shape
    return pl.pallas_call(
        near_kernel,
        grid=(rows // TILE,),
        out_shape=jax.ShapeDtypeStruct(residual.shape, jnp.float32),
        in_specs=[tiles(near_blocks.shape[1]), WHOLE, tiles(width)],
        out_specs=tiles(width),
        scratch_shapes=[pltpu.VMEM((rows + 2 * HALO, width), jnp.bfloat16)],
        cost_estimate=pl.CostEstimate(
            flops=2 * rows * near_blocks.shape[1] * width, bytes_accessed=2 * near_blocks.size + 8 * residual.size, transcendentals=0
        ),
        name="near",
    )(near_blocks, vb, residual)


def image_kernel(fanout, list_ref, base_ref, res_ref, incoming_ref, coupling_ref, target_ref, first_ref, last_ref, before_ref, after_ref, image_ref, part_ref, cross):
    i = pl.program_id(0)
    width = base_ref.shape[1]
    half = width // 2
    leaves = IMAGE_TILE // LEAF

    @pl.when(i == 0)
    def _():
        part_ref[...] = jnp.zeros_like(part_ref)
        cross[...] = jnp.zeros_like(cross)

    for l in range(leaves):
        trans = 0.0
        for f in range(fanout):
            trans = trans + dot16(coupling_ref[l, f], incoming_ref[list_ref[(i * leaves + l) * fanout + f]])
        far = tdot16(target_ref[:, l * LEAF : (l + 1) * LEAF], trans.astype(jnp.bfloat16))
        image_ref[l * LEAF : (l + 1) * LEAF] = base_ref[l * LEAF : (l + 1) * LEAF] + far

    @pl.when(i < NEAR // IMAGE_TILE)
    def _():
        image_ref[...] += dot16(first_ref[...], before_ref[...])

    @pl.when(i >= pl.num_programs(0) - NEAR // IMAGE_TILE)
    def _():
        image_ref[...] += dot16(last_ref[...], after_ref[...])

    high, low = split(image_ref[...])
    res_high, res_low = split(res_ref[...])
    sums = tdot16(high, jnp.concatenate([high, low, res_high, res_low], axis=1))
    gram = sums[:, :width]
    proj = sums[:, 2 * width : 3 * width] + sums[:, 3 * width :] + tdot16(low, res_high)
    cross[...] += sums[:, width : 2 * width]
    part_ref[:width] += gram[:, :half]
    part_ref[width : 2 * width] += gram[:, half:]
    part_ref[2 * width : 3 * width] += proj[:, :half]
    part_ref[3 * width :] += proj[:, half:]

    @pl.when(i == pl.num_programs(0) - 1)
    def _():
        both = cross[...] + cross[...].T
        part_ref[:width] += both[:, :half]
        part_ref[width : 2 * width] += both[:, half:]


def image_and_sums(readers, base, residual, incoming, coupling, target_t, near_blocks, before, after):
    rows, width = residual.shape
    leaves, fanout, rank, _ = coupling.shape
    step = IMAGE_TILE // LEAF
    edge, steps = NEAR // IMAGE_TILE, rows // IMAGE_TILE
    last_column = near_blocks.shape[1] // HALO - 1
    return pl.pallas_call(
        functools.partial(image_kernel, fanout),
        grid=(rows // IMAGE_TILE,),
        out_shape=(
            jax.ShapeDtypeStruct(residual.shape, jnp.float32),
            jax.ShapeDtypeStruct((4 * width, width // 2), jnp.float32),
        ),
        in_specs=[
            pl.BlockSpec(memory_space=pltpu.SMEM),
            tiles(width, IMAGE_TILE),
            tiles(width, IMAGE_TILE),
            WHOLE,
            pl.BlockSpec((step, fanout, rank, rank), lambda i: (i, 0, 0, 0)),
            pl.BlockSpec((rank, IMAGE_TILE), lambda i: (0, i)),
            pl.BlockSpec((IMAGE_TILE, HALO), lambda i: (jnp.minimum(i, edge - 1), 0)),
            pl.BlockSpec((IMAGE_TILE, HALO), lambda i: (jnp.maximum(i, steps - edge), last_column)),
            WHOLE,
            WHOLE,
        ],
        out_specs=(tiles(width, IMAGE_TILE), pl.BlockSpec((4 * width, width // 2), lambda i: (0, 0))),
        scratch_shapes=[pltpu.VMEM((width, width), jnp.float32)],
        name="image",
    )(readers, base, residual, incoming, coupling, target_t, near_blocks, near_blocks, before, after)


def product(x, alpha_ref):
    high, low = split(x)
    a_high, a_low = split(alpha_ref[...])
    return dot16(high, a_high) + dot16(high, a_low) + dot16(low, a_high)


def update_kernel(res_ref, image_ref, alpha_ref, source_ref, new_ref, vb_ref, coef_ref):
    new = res_ref[...] - product(image_ref[...], alpha_ref)
    new_ref[...] = new
    vb = new.astype(jnp.bfloat16)
    vb_ref[...] = vb
    for l in range(TILE // LEAF):
        leaf = slice(l * LEAF, (l + 1) * LEAF)
        coef_ref[l] = dot16(source_ref[:, leaf], vb[leaf]).astype(jnp.bfloat16)


def update(residual, image, alpha, source_t):
    rows, width = residual.shape
    rank, step = source_t.shape[0], TILE // LEAF
    return pl.pallas_call(
        update_kernel,
        grid=(rows // TILE,),
        out_shape=(
            jax.ShapeDtypeStruct(residual.shape, jnp.float32),
            jax.ShapeDtypeStruct(residual.shape, jnp.bfloat16),
            jax.ShapeDtypeStruct((rows // LEAF, rank, width), jnp.bfloat16),
        ),
        in_specs=[tiles(width), tiles(width), WHOLE, pl.BlockSpec((rank, TILE), lambda i: (0, i))],
        out_specs=(tiles(width), tiles(width), pl.BlockSpec((step, rank, width), lambda i: (i, 0, 0))),
        name="update",
    )(residual, image, alpha, source_t)


def last_kernel(count, *refs):
    residuals, alphas, image_ref = refs[:count], refs[count : 2 * count], refs[2 * count]
    sol_ref, new_ref = refs[2 * count + 1 :]
    total = product(residuals[0][...], alphas[0])
    for res_ref, alpha_ref in zip(residuals[1:], alphas[1:]):
        total = total + product(res_ref[...], alpha_ref)
    sol_ref[...] = total
    new_ref[...] = residuals[-1][...] - product(image_ref[...], alphas[-1])


def last_update(residuals, alphas, image):
    rows, width = image.shape
    count = len(residuals)
    shape = jax.ShapeDtypeStruct(image.shape, jnp.float32)
    return pl.pallas_call(
        functools.partial(last_kernel, count),
        grid=(rows // TILE,),
        out_shape=(shape, shape),
        in_specs=[tiles(width)] * count + [WHOLE] * count + [tiles(width)],
        out_specs=(tiles(width), tiles(width)),
        name="last_update",
    )(*residuals, *alphas, image)


def shards(rhs, near_blocks, source_basis, target_basis, far_coupling, send_ids, far_list):
    rows, width = rhs.shape
    rank = source_basis.shape[1]
    leaves = rows // LEAF
    senders = send_ids[0].reshape(-1)
    readers = far_list[0]
    source_leaf = source_basis.reshape(leaves, LEAF, rank)
    target_t = target_basis.T
    n_blk = lax.axis_size("blk")
    n = lax.axis_size("wide") * n_blk
    residual = rhs
    vb = rhs.astype(jnp.bfloat16)
    coef = jnp.einsum(
        "lia,lis->las", source_leaf, vb.reshape(leaves, LEAF, width), preferred_element_type=jnp.float32
    ).astype(jnp.bfloat16)
    residuals, alphas = [], []
    for step in range(ITERS):
        outgoing = coef[senders]
        incoming = lax.all_to_all(
            outgoing, ("wide", "blk"), split_axis=0, concat_axis=0, tiled=True
        )
        before, after = sides(vb, "blk", HALO)
        base = near_base(near_blocks, vb, residual)
        image, part = image_and_sums(
            readers, base, residual, incoming, far_coupling, target_t, near_blocks, before, after
        )
        both = sum_over_devices(part, n, n_blk)
        residuals.append(residual)
        alphas.append(solve(both, width))
        if step < ITERS - 1:
            residual, vb, coef = update(residual, image, alphas[-1], source_basis.T)
    return last_update(residuals, alphas, image)


def solution(mesh):
    in_specs = (
        P(("wide", "blk"), None),
        P(("wide", "blk"), None),
        P(("wide", "blk"), None),
        P(("wide", "blk"), None),
        P(("wide", "blk"), None, None, None),
        P(("wide", "blk"), None, None),
        P(("wide", "blk"), None),
    )
    out_specs = (P(("wide", "blk"), None), P(("wide", "blk"), None))
    return jax.shard_map(shards, mesh=mesh, in_specs=in_specs, out_specs=out_specs, check_vma=False)
```
